256 devices in a mesh: path: 32 (over y, x, core), fac: 8 (over z).
Axes of the slice: x: 4, y: 4, z: 8, core: 2. Of those that a mesh axis runs over, the one named last changes fastest.
Arguments:
- shocks: bfloat16 [4, 2048, 8192], P(None, 'path', 'fac'), may hold values from -6 to 6
- chol_factor: bfloat16 [8192, 8192], P('path', 'fac')
- factor_vol: float32 [8192], P('fac'), may hold values from 0.3 to 1.5
- trade_loading: bfloat16 [8192, 4096], P(None, 'fac'), may hold values from -0.0625 to 0.0625
- basis_loading: bfloat16 [8192, 64], replicated, may hold values from -0.0625 to 0.0625
- trade_set: int32 [4096], P('fac'), may hold values from 0 to 4095, as said below
Outputs:
- exposure: float32 [4, 2048, 4096], P(None, 'path', 'fac')
The draws below stay inside these ranges and needn't reach their ends.
Inputs may be any that keep to these rules, and one draw needn't show every extreme that they name: Each trade belongs to a netting set of its own block: trade_set[k] // 512 equals k // 512.
All inputs are finite; a program needn't handle non-finite values.
Results may differ from the reference program's by a relative error of at most 0.0047.
Values may be sent and summed in bfloat16 or wider, within the bound.
A program may use at most 128 MiB of HBM per device.

```python
import math
import jax
import jax.numpy as jnp
from jax import lax

F = 8192
NSETS = 4096
NB = 64
STEPS = 4
TR_DEV = 512
PATHS = 2048
TRADES = 4096
NS_DEV = 512


def draw_chol_factor(key, part):
    row_index = lax.broadcasted_iota(jnp.int32, (F, F), 0)
    col_index = lax.broadcasted_iota(jnp.int32, (F, F), 1)
    noise = jax.random.normal(key, (F, F), jnp.float32)
    scale = 1.0 / jnp.sqrt(jnp.maximum(row_index, 1).astype(jnp.float32))
    lower = jnp.where(col_index < row_index, noise * scale, 0.0)
    return jnp.where(row_index == col_index, 1.0, lower).astype(jnp.bfloat16)


def draw_trade_set(key, part):
    trade_index = jnp.arange(TRADES, dtype=jnp.int32)
    block_index = trade_index // TR_DEV
    within = trade_index % TR_DEV
    local_set = jax.random.randint(key, (TRADES,), 0, NS_DEV, dtype=jnp.int32)
    local_set = jnp.where(within == 0, 0, jnp.where(within == 1, NS_DEV - 1, local_set))
    return (block_index * NS_DEV + local_set).astype(jnp.int32)


def block_levels(stream_key, shape, cuts, smallest, largest):
    level = 1.0
    for axis_at, parts in cuts:
        heights = jax.random.uniform(jax.random.fold_in(jax.random.fold_in(stream_key, 6), axis_at), (parts,), jnp.float32, smallest / len(cuts), largest / len(cuts))
        level = level * jnp.repeat(jnp.exp(heights), shape[axis_at] // parts).reshape((-1,) + (1,) * (len(shape) - 1 - axis_at))
    return level


def centred(rng, dims, deviation, limit, split=(), kind=jnp.bfloat16):
    entries = deviation * jax.random.normal(rng, dims, jnp.float32)
    if split:
        entries = entries * block_levels(rng, dims, split, -0.22, 0.18)
    return jnp.clip(entries, -limit, limit).astype(kind)


def setup_inputs(seed: int = 0) -> dict:
    seeds = jax.random.split(jax.random.key(seed), 7)
    shocks = centred(seeds[0], (STEPS, PATHS, F), 1.0, 6.0, ((1, 32), (2, 8)))
    chol_factor = draw_chol_factor(jax.random.fold_in(seeds[6], 71), 0)
    factor_vol = jnp.clip(jnp.exp(math.log(1.5) - 1.60943787 * jax.random.uniform(seeds[2], (F,), jnp.float32) ** block_levels(seeds[2], (F,), ((0, 8),), -0.2, 0.2)), 0.3, 1.5)
    trade_loading = centred(seeds[3], (F, TRADES), F ** -0.5, 0.0625, ((1, 8),))
    basis_loading = centred(seeds[4], (F, NB), F ** -0.5, 0.0625)
    trade_set = draw_trade_set(jax.random.fold_in(seeds[6], 71), 0)
    return {"shocks": shocks, "chol_factor": chol_factor, "factor_vol": factor_vol, "trade_loading": trade_loading, "basis_loading": basis_loading, "trade_set": trade_set}


def solve_step(gram, moment, basis, total_paths):
    ridged = gram + 0.01 * total_paths * jnp.eye(gram.shape[0], dtype=jnp.float32)
    factor = jnp.linalg.cholesky(ridged)
    coef = jax.scipy.linalg.cho_solve((factor, True), moment)
    predicted = jnp.dot(basis.astype(jnp.float32), coef.astype(jnp.float32), precision=lax.Precision.HIGHEST, preferred_element_type=jnp.float32)
    return jnp.maximum(predicted, 0.0)

def reference(shocks, chol_factor, factor_vol, trade_loading, basis_loading, trade_set):
    flat_shocks = shocks.reshape(STEPS * PATHS, F)
    increments = jnp.dot(flat_shocks.astype(jnp.float32), chol_factor.T.astype(jnp.float32), preferred_element_type=jnp.float32)
    scaled = increments.reshape(STEPS, PATHS, F) * (factor_vol / math.sqrt(STEPS))
    levels = jnp.cumsum(scaled, axis=0).astype(jnp.bfloat16).reshape(STEPS * PATHS, F)
    drivers = jnp.dot(levels.astype(jnp.float32), trade_loading.astype(jnp.float32), preferred_element_type=jnp.float32)
    projected = jnp.dot(levels.astype(jnp.float32), basis_loading.astype(jnp.float32), preferred_element_type=jnp.float32)
    values = jax.nn.softplus(drivers) - 1.0
    member = (trade_set[:, None] == jnp.arange(NSETS, dtype=jnp.int32)[None, :]).astype(jnp.float32)
    netting = jnp.dot(values.astype(jnp.float32), member.astype(jnp.float32), precision=lax.Precision.HIGHEST, preferred_element_type=jnp.float32)
    basis = jnp.tanh(projected).reshape(STEPS, PATHS, NB)
    netting = netting.reshape(STEPS, PATHS, NSETS)
    results = []
    for step in range(STEPS):
        step_basis = basis[step]
        gram = jnp.dot(step_basis.T.astype(jnp.float32), step_basis.astype(jnp.float32), precision=lax.Precision.HIGHEST, preferred_element_type=jnp.float32)
        moment = jnp.dot(step_basis.T.astype(jnp.float32), netting[step].astype(jnp.float32), precision=lax.Precision.HIGHEST, preferred_element_type=jnp.float32)
        results.append(solve_step(gram, moment, step_basis, PATHS))
    return jnp.stack(results)
```

```python
import functools
import math

import jax
import jax.numpy as jnp
from jax import lax
from jax.experimental import pallas as pl
from jax.experimental.pallas import tpu as pltpu
from jax.sharding import PartitionSpec as P

F = 8192
NSETS = 4096
MESH = pl.DeviceIdType.MESH
HIGH = lax.Precision.HIGHEST


def split_dot(a, b):
    high = a.astype(jnp.bfloat16)
    low = (a - high.astype(jnp.float32)).astype(jnp.bfloat16)
    both = jnp.dot(
        jnp.concatenate([high, low], axis=0), b, preferred_element_type=jnp.float32
    )
    rows = a.shape[0]
    return both[:rows] + both[rows:]


def invert(mats):
    n = mats[0].shape[0]
    count = len(mats)
    row = lax.broadcasted_iota(jnp.int32, (n, 2 * n), 0)
    lane = lax.broadcasted_iota(jnp.int32, (n, 2 * n), 1)
    eye = jnp.where(lane == row + n, 1.0, 0.0)
    wide = [jnp.concatenate([m, jnp.zeros_like(m)], axis=1) + eye for m in mats]
    blocks = tuple(tuple(w[8 * b : 8 * b + 8] for b in range(n // 8)) for w in wide)
    sub = lax.broadcasted_iota(jnp.int32, (8, 1), 0)

    def body(_, blocks):
        done = []
        for m in range(count):
            rows = list(blocks[m])
            for k in range(8):
                pivot_row = rows[0][k : k + 1, :]
                inverse = 1.0 / pivot_row[:, k : k + 1]
                scaled = pivot_row * inverse
                fresh = []
                for b in range(n // 8):
                    col = rows[b][:, k : k + 1]
                    if b == 0:
                        col = jnp.where(sub == k, col - 1.0, col)
                    fresh.append(rows[b] - col * scaled)
                rows = fresh
            rows = rows[1:] + rows[:1]
            done.append(tuple(pltpu.roll(r, 2 * n - 8, 1) for r in rows))
        return tuple(done)

    blocks = lax.fori_loop(0, n // 8, body, blocks)
    return [jnp.concatenate(b, axis=0)[:, :n] for b in blocks]


def tail_kernel(
    group, total_paths, drive_ref, proj_ref, member_ref, out_ref,
    part, landed, total, base, send_a, recv_a, send_b, recv_b,
):
    me = lax.axis_index("path")
    barrier = pltpu.get_barrier_semaphore()

    @pl.loop(1, group)
    def _(d):
        pl.semaphore_signal(
            barrier, inc=1, device_id={"path": lax.rem(me + d, group)}, device_id_type=MESH
        )

    steps, paths, sets = drive_ref.shape
    nb = proj_ref.shape[2]
    contract = (((0,), (0,)), ((), ()))
    for t in range(steps):
        v = drive_ref[t]
        values = jnp.maximum(v, 0.0) + jnp.log(1.0 + jnp.exp(-jnp.abs(v))) - 1.0
        basis = jnp.tanh(proj_ref[t])
        base[t] = basis
        moment = lax.dot_general(
            basis, values, contract, precision=HIGH, preferred_element_type=jnp.float32
        )
        gram = lax.dot_general(
            basis, basis, contract, precision=HIGH, preferred_element_type=jnp.float32
        )
        gram = jnp.concatenate([gram, jnp.zeros_like(gram)], axis=1)
        at = pl.ds(t * nb // 8, nb // 8)
        part[at, :, 0:sets] = moment.reshape(nb // 8, 8, sets)
        part[at, :, sets : sets + 2 * nb] = gram.reshape(nb // 8, 8, 2 * nb)

    pl.semaphore_wait(barrier, group - 1)

    def out_copy(d):
        to = lax.rem(me + d, group)
        return pltpu.make_async_remote_copy(
            src_ref=part.at[to], dst_ref=landed.at[me], send_sem=send_a.at[to],
            recv_sem=recv_a.at[me], device_id={"path": to}, device_id_type=MESH,
        )

    def in_copy(d):
        source = lax.rem(me + d, group)
        return pltpu.make_async_remote_copy(
            src_ref=part.at[source], dst_ref=landed.at[source], send_sem=send_a.at[source],
            recv_sem=recv_a.at[source], device_id={"path": source}, device_id_type=MESH,
        )

    @pl.loop(1, group)
    def _(d):
        out_copy(d).start()

    landed[me] = part[me]

    @pl.loop(1, group)
    def _(d):
        in_copy(d).wait()

    mine = jnp.sum(landed[...], axis=0)
    total[me, :, 0:sets] = split_dot(mine[:, 0:sets], member_ref[...])
    total[me, :, sets : sets + 2 * nb] = mine[:, sets : sets + 2 * nb]

    def share_copy(d):
        to = lax.rem(me + d, group)
        return pltpu.make_async_remote_copy(
            src_ref=total.at[me], dst_ref=total.at[me], send_sem=send_b.at[to],
            recv_sem=recv_b.at[me], device_id={"path": to}, device_id_type=MESH,
        )

    def taken_copy(d):
        source = lax.rem(me + d, group)
        return pltpu.make_async_remote_copy(
            src_ref=total.at[source], dst_ref=total.at[source], send_sem=send_b.at[source],
            recv_sem=recv_b.at[source], device_id={"path": source}, device_id_type=MESH,
        )

    @pl.loop(1, group)
    def _(d):
        share_copy(d).start()

    @pl.loop(1, group)
    def _(d):
        taken_copy(d).wait()

    row = lax.broadcasted_iota(jnp.int32, (nb, nb), 0)
    lane = lax.broadcasted_iota(jnp.int32, (nb, nb), 1)
    ridge = jnp.where(row == lane, 0.01 * total_paths, 0.0)
    grams = [
        total[t * nb // 8 : (t + 1) * nb // 8, :, sets : sets + nb].reshape(nb, nb) + ridge
        for t in range(steps)
    ]
    inverses = invert(grams)
    for t in range(steps):
        weight = jnp.dot(
            base[t], inverses[t], precision=HIGH, preferred_element_type=jnp.float32
        )
        moment = total[t * nb // 8 : (t + 1) * nb // 8, :, 0:sets].reshape(nb, sets)
        predicted = jnp.dot(
            weight, moment, precision=HIGH, preferred_element_type=jnp.float32
        )
        out_ref[t] = jnp.maximum(predicted, 0.0)


def tail(drive, proj, member, total_paths):
    group = lax.axis_size("path")
    steps, paths, sets = drive.shape
    nb = proj.shape[2]
    rows = steps * nb // 8
    width = sets + 2 * nb
    vmem = pl.BlockSpec(memory_space=pltpu.VMEM)
    return pl.pallas_call(
        functools.partial(tail_kernel, group, total_paths),
        out_shape=jax.ShapeDtypeStruct(drive.shape, jnp.float32),
        in_specs=[vmem] * 3,
        out_specs=vmem,
        scratch_shapes=[
            pltpu.VMEM((rows, 8, width), jnp.float32),
            pltpu.VMEM((group, 8, width), jnp.float32),
            pltpu.VMEM((rows, 8, width), jnp.float32),
            pltpu.VMEM((steps, paths, nb), jnp.float32),
            pltpu.SemaphoreType.DMA((group,)),
            pltpu.SemaphoreType.DMA((group,)),
            pltpu.SemaphoreType.DMA((group,)),
            pltpu.SemaphoreType.DMA((group,)),
        ],
        compiler_params=pltpu.CompilerParams(collective_id=1, has_side_effects=True),
    )(drive, proj, member)


def on_device(shocks, chol_factor, factor_vol, trade_loading, basis_loading, trade_set):
    step_count, path_count, fac_width = shocks.shape
    row_count = step_count * path_count
    flat_shocks = shocks.reshape(row_count, fac_width)
    factor_share = F // lax.axis_size("fac")
    contract_last = (((1,), (1,)), ((), ()))
    full_rows = lax.all_gather(chol_factor, "path", axis=0, tiled=True)
    increments = lax.psum_scatter(
        lax.dot_general(full_rows, flat_shocks, contract_last, preferred_element_type=jnp.float32),
        "fac",
        scatter_dimension=0,
        tiled=True,
    )
    scaled = increments.reshape(factor_share, step_count, path_count) * (
        factor_vol[:, None, None] / math.sqrt(step_count)
    )
    levels = jnp.cumsum(scaled, axis=1).astype(jnp.bfloat16).reshape(factor_share, row_count)
    basis_count = basis_loading.shape[1]
    contract_first = (((0,), (0,)), ((), ()))
    piece = lax.all_gather(levels, "fac", axis=0, tiled=True)
    trade_sum = lax.dot_general(
        piece, trade_loading, contract_first, preferred_element_type=jnp.float32
    )
    basis_sum = lax.dot_general(
        piece, basis_loading, contract_first, preferred_element_type=jnp.float32
    )
    sets_here = NSETS // lax.axis_size("fac")
    local_set = trade_set % sets_here
    member = (local_set[:, None] == jnp.arange(sets_here, dtype=jnp.int32)[None, :]).astype(
        jnp.bfloat16
    )
    drive = trade_sum.reshape(step_count, path_count, -1)
    proj = basis_sum.reshape(step_count, path_count, basis_count)
    return tail(drive, proj, member, path_count * lax.axis_size("path"))


def solution(mesh):
    in_specs = (P(None, "path", "fac"), P("path", "fac"), P("fac"), P(None, "fac"), P(), P("fac"))
    out_specs = P(None, "path", "fac")
    return jax.shard_map(
        on_device, mesh=mesh, in_specs=in_specs, out_specs=out_specs, check_vma=False
    )
```

```python
import functools
import math

import jax
import jax.numpy as jnp
from jax import lax
from jax.experimental import pallas as pl
from jax.experimental.pallas import tpu as pltpu
from jax.sharding import PartitionSpec as P

NSETS = 4096
MESH = pl.DeviceIdType.MESH
HIGH = lax.Precision.HIGHEST


def split_dot(a, b):
    high = a.astype(jnp.bfloat16)
    low = (a - high.astype(jnp.float32)).astype(jnp.bfloat16)
    both = jnp.dot(
        jnp.concatenate([high, low], axis=0), b, preferred_element_type=jnp.float32
    )
    rows = a.shape[0]
    return both[:rows] + both[rows:]


def invert(mats):
    n = mats[0].shape[0]
    count = len(mats)
    row = lax.broadcasted_iota(jnp.int32, (n, 2 * n), 0)
    lane = lax.broadcasted_iota(jnp.int32, (n, 2 * n), 1)
    eye = jnp.where(lane == row + n, 1.0, 0.0)
    wide = [jnp.concatenate([m, jnp.zeros_like(m)], axis=1) + eye for m in mats]
    blocks = tuple(tuple(w[8 * b : 8 * b + 8] for b in range(n // 8)) for w in wide)
    sub = lax.broadcasted_iota(jnp.int32, (8, 1), 0)

    def body(_, blocks):
        done = []
        for m in range(count):
            rows = list(blocks[m])
            for k in range(8):
                pivot_row = rows[0][k : k + 1, :]
                inverse = 1.0 / pivot_row[:, k : k + 1]
                scaled = pivot_row * inverse
                fresh = []
                for b in range(n // 8):
                    col = rows[b][:, k : k + 1]
                    if b == 0:
                        col = jnp.where(sub == k, col - 1.0, col)
                    fresh.append(rows[b] - col * scaled)
                rows = fresh
            rows = rows[1:] + rows[:1]
            done.append(tuple(pltpu.roll(r, 2 * n - 8, 1) for r in rows))
        return tuple(done)

    blocks = lax.fori_loop(0, n // 8, body, blocks)
    return [jnp.concatenate(b, axis=0)[:, :n] for b in blocks]


def tail_kernel(
    group, total_paths, drive_ref, proj_ref, member_ref, out_ref,
    part, landed, total, base, send_a, recv_a, send_b, recv_b,
):
    me = lax.axis_index("path")
    barrier = pltpu.get_barrier_semaphore()

    @pl.loop(1, group)
    def _(d):
        pl.semaphore_signal(
            barrier, inc=1, device_id={"path": lax.rem(me + d, group)}, device_id_type=MESH
        )

    steps, paths, sets = drive_ref.shape
    nb = proj_ref.shape[2]
    contract = (((0,), (0,)), ((), ()))
    v = jnp.zeros(drive_ref.shape[1:], jnp.float32)
    w = jnp.zeros(proj_ref.shape[1:], jnp.float32)
    for t in range(steps):
        v = v + drive_ref[t]
        w = w + proj_ref[t]
        values = jnp.maximum(v, 0.0) + jnp.log(1.0 + jnp.exp(-jnp.abs(v))) - 1.0
        basis = jnp.tanh(w)
        base[t] = basis
        moment = lax.dot_general(
            basis, values, contract, precision=HIGH, preferred_element_type=jnp.float32
        )
        gram = lax.dot_general(
            basis, basis, contract, precision=HIGH, preferred_element_type=jnp.float32
        )
        gram = jnp.concatenate([gram, jnp.zeros_like(gram)], axis=1)
        at = pl.ds(t * nb // 8, nb // 8)
        part[at, :, 0:sets] = moment.reshape(nb // 8, 8, sets)
        part[at, :, sets : sets + 2 * nb] = gram.reshape(nb // 8, 8, 2 * nb)

    pl.semaphore_wait(barrier, group - 1)

    def out_copy(d):
        to = lax.rem(me + d, group)
        return pltpu.make_async_remote_copy(
            src_ref=part.at[to], dst_ref=landed.at[me], send_sem=send_a.at[to],
            recv_sem=recv_a.at[me], device_id={"path": to}, device_id_type=MESH,
        )

    def in_copy(d):
        source = lax.rem(me + d, group)
        return pltpu.make_async_remote_copy(
            src_ref=part.at[source], dst_ref=landed.at[source], send_sem=send_a.at[source],
            recv_sem=recv_a.at[source], device_id={"path": source}, device_id_type=MESH,
        )

    @pl.loop(1, group)
    def _(d):
        out_copy(d).start()

    landed[me] = part[me]

    @pl.loop(1, group)
    def _(d):
        in_copy(d).wait()

    mine = jnp.sum(landed[...], axis=0)
    total[me, :, 0:sets] = split_dot(mine[:, 0:sets], member_ref[...])
    total[me, :, sets : sets + 2 * nb] = mine[:, sets : sets + 2 * nb]

    def share_copy(d):
        to = lax.rem(me + d, group)
        return pltpu.make_async_remote_copy(
            src_ref=total.at[me], dst_ref=total.at[me], send_sem=send_b.at[to],
            recv_sem=recv_b.at[me], device_id={"path": to}, device_id_type=MESH,
        )

    def taken_copy(d):
        source = lax.rem(me + d, group)
        return pltpu.make_async_remote_copy(
            src_ref=total.at[source], dst_ref=total.at[source], send_sem=send_b.at[source],
            recv_sem=recv_b.at[source], device_id={"path": source}, device_id_type=MESH,
        )

    @pl.loop(1, group)
    def _(d):
        share_copy(d).start()

    @pl.loop(1, group)
    def _(d):
        taken_copy(d).wait()

    row = lax.broadcasted_iota(jnp.int32, (nb, nb), 0)
    lane = lax.broadcasted_iota(jnp.int32, (nb, nb), 1)
    ridge = jnp.where(row == lane, 0.01 * total_paths, 0.0)
    grams = [
        total[t * nb // 8 : (t + 1) * nb // 8, :, sets : sets + nb].reshape(nb, nb) + ridge
        for t in range(steps)
    ]
    inverses = invert(grams)
    for t in range(steps):
        weight = jnp.dot(
            base[t], inverses[t], precision=HIGH, preferred_element_type=jnp.float32
        )
        moment = total[t * nb // 8 : (t + 1) * nb // 8, :, 0:sets].reshape(nb, sets)
        predicted = jnp.dot(
            weight, moment, precision=HIGH, preferred_element_type=jnp.float32
        )
        out_ref[t] = jnp.maximum(predicted, 0.0)


def tail(drive, proj, member, total_paths):
    group = lax.axis_size("path")
    steps, paths, sets = drive.shape
    nb = proj.shape[2]
    rows = steps * nb // 8
    width = sets + 2 * nb
    vmem = pl.BlockSpec(memory_space=pltpu.VMEM)
    return pl.pallas_call(
        functools.partial(tail_kernel, group, total_paths),
        out_shape=jax.ShapeDtypeStruct(drive.shape, jnp.float32),
        in_specs=[vmem] * 3,
        out_specs=vmem,
        scratch_shapes=[
            pltpu.VMEM((rows, 8, width), jnp.float32),
            pltpu.VMEM((group, 8, width), jnp.float32),
            pltpu.VMEM((rows, 8, width), jnp.float32),
            pltpu.VMEM((steps, paths, nb), jnp.float32),
            pltpu.SemaphoreType.DMA((group,)),
            pltpu.SemaphoreType.DMA((group,)),
            pltpu.SemaphoreType.DMA((group,)),
            pltpu.SemaphoreType.DMA((group,)),
        ],
        compiler_params=pltpu.CompilerParams(collective_id=1, has_side_effects=True),
    )(drive, proj, member)


def push(src, dst, send_sem, recv_sem, where):
    return pltpu.make_async_remote_copy(
        src_ref=src, dst_ref=dst, send_sem=send_sem, recv_sem=recv_sem,
        device_id=where, device_id_type=MESH,
    )


def rises(s):
    extra = [0, 1, 3, 3, 0, 1, 1, 0]
    total = 2
    for at, more in enumerate(extra):
        if more:
            total = total + jnp.where(s == at, more, 0)
    return total


def front_kernel(
    planes, group, scale, chol_ref, shock_hbm, vol_ref, trade_hbm, basis_ref, drive_ref, proj_ref,
    turned, slices, shocks, vols, loads, full, acc,
    local_sem, a_send, a_recv, v_send, v_recv, s_up, s_down, s_recv,
    c_up, c_down, c_recv, g_send, g_recv,
):
    me = lax.axis_index("path")
    z = lax.axis_index("fac")
    above, below = {"fac": lax.rem(z + 1, planes)}, {"fac": lax.rem(z + planes - 1, planes)}
    per_plane = group // planes
    height, cols = chol_ref.shape
    width = cols // group
    sets = trade_hbm.shape[1]
    nb = basis_ref.shape[1]
    half_rows = shock_hbm.shape[0] // 2

    barrier = pltpu.get_barrier_semaphore()

    @pl.loop(1, group)
    def _(d):
        pl.semaphore_signal(
            barrier, inc=1, device_id={"path": lax.rem(me + d, group)}, device_id_type=MESH
        )

    @pl.loop(1, planes)
    def _(d):
        pl.semaphore_signal(
            barrier, inc=1, device_id={"fac": lax.rem(z + d, planes)}, device_id_type=MESH
        )

    load_trades = pltpu.make_async_copy(trade_hbm, loads.at[:, 0:sets], local_sem.at[0])
    load_trades.start()
    load_shocks = [
        pltpu.make_async_copy(
            shock_hbm.at[pl.ds(h * half_rows, half_rows)], shocks.at[z, h], local_sem.at[1 + h]
        )
        for h in range(2)
    ]
    for copy in load_shocks:
        copy.start()

    for b in range(cols // 128):
        block = chol_ref[:, 128 * b : 128 * (b + 1)].T
        at = pl.ds(b * (128 // width), 128 // width)
        turned[at] = block.reshape(128 // width, width, height)
    vols[z] = vol_ref[...]
    for copy in load_shocks:
        copy.wait()

    pl.semaphore_wait(barrier, group - 1 + planes - 1)

    def shock_up(s, h):
        return push(shocks.at[s, h], shocks.at[s, h], s_up.at[s * 2 + h], s_recv.at[s * 2 + h], above)

    def shock_down(s, h):
        return push(
            shocks.at[s, h], shocks.at[s, h], s_down.at[s * 2 + h], s_recv.at[s * 2 + h], below
        )

    def up_source(k):
        return lax.rem(z + planes - k, planes)

    def down_source(k):
        return lax.rem(z + k, planes)

    for h in range(2):
        shock_up(z, h).start()
        shock_down(z, h).start()

    def vol_copy(d):
        to = lax.rem(z + d, planes)
        return push(vols.at[z], vols.at[z], v_send.at[to], v_recv.at[z], {"fac": to})

    def vol_taken(d):
        source = lax.rem(z + d, planes)
        return push(
            vols.at[source], vols.at[source], v_send.at[source], v_recv.at[source], {"fac": source}
        )

    @pl.loop(1, planes)
    def _(d):
        vol_copy(d).start()

    def slice_copy(d):
        to = lax.rem(me + d, group)
        return push(turned.at[to], slices.at[me, z], a_send.at[to], a_recv.at[me], {"path": to})

    def slice_taken(source):
        return push(
            turned.at[source], slices.at[source, z], a_send.at[source], a_recv.at[source],
            {"path": source},
        )

    @pl.when(me >= per_plane * z)
    def _():
        @pl.loop(1, group)
        def _(d):
            slice_copy(d).start()

        slices[me, z] = turned[me]

    @pl.loop(1, planes)
    def _(d):
        vol_taken(d).wait_recv()

    load_trades.wait()
    vol_rows = vols[...].reshape(planes * vol_ref.shape[0], 128) * scale
    vol_rows = jnp.concatenate(
        [vol_rows, jnp.zeros((128 - vol_rows.shape[0], 128), jnp.float32)], axis=0
    )

    def scale_rows(c, columns):
        column = columns[:, 0:1]
        at = pl.ds(pl.multiple_of(c * 128, 128), 128)
        loads[at, 0:sets] = (loads[at, 0:sets].astype(jnp.float32) * column).astype(jnp.bfloat16)
        basis = basis_ref[at, :].astype(jnp.float32) * column
        high = basis.astype(jnp.bfloat16)
        low = (basis - high.astype(jnp.float32)).astype(jnp.bfloat16)
        loads[at, sets : sets + 2 * nb] = jnp.concatenate([high, low], axis=1)
        return pltpu.roll(columns, 127, 1)

    lax.fori_loop(0, loads.shape[0] // 128, scale_rows, vol_rows.T)

    @pl.loop(1, group)
    def _(d):
        source = lax.rem(me + d, group)

        @pl.when(source >= per_plane * z)
        def _():
            slice_taken(source).wait_recv()

    def part(s, g):
        return slices.at[pl.ds(g * per_plane, per_plane), s]

    def slice_up(s, g):
        return push(part(s, g), part(s, g), c_up.at[s * planes + g], c_recv.at[s * planes + g], above)

    def slice_down(s, g):
        return push(
            part(s, g), part(s, g), c_down.at[s * planes + g], c_recv.at[s * planes + g], below
        )

    @pl.loop(0, planes)
    def _(g):
        @pl.when(g >= z)
        def _():
            slice_up(z, g).start()
            slice_down(z, g).start()

    @pl.loop(1, 6)
    def _(k):
        low, high = up_source(k), down_source(k)
        rise, fall = rises(low), planes - 1 - rises(high)

        @pl.loop(0, planes)
        def _(g):
            @pl.when((g >= low) & (k <= rise))
            def _():
                slice_up(low, g).wait_recv()

                @pl.when(k < rise)
                def _():
                    slice_up(low, g).start()

            @pl.when((g >= high) & (k <= fall))
            def _():
                slice_down(high, g).wait_recv()

                @pl.when(k < fall)
                def _():
                    slice_down(high, g).start()

    def shock_step(k):
        for h in range(2):
            shock_up(up_source(k), h).wait_recv()
            shock_down(down_source(k), h).wait_recv()
            if k < 3 or h == 0:
                shock_up(up_source(k), h).start()
            if k < 3 or h == 1:
                shock_down(down_source(k), h).start()

    shock_step(1)

    acc[...] = jnp.zeros_like(acc)
    for g in reversed(range(planes)):
        rows = (g + 1) * width

        def add(q, _):
            left = slices[q, 0 : g + 1].reshape(rows, height)
            at = pl.ds(pl.multiple_of(q * height, height), height)
            acc[0:rows] += jnp.dot(left, loads[at, :], preferred_element_type=jnp.float32)
            return 0

        lax.fori_loop(g * per_plane, (g + 1) * per_plane, add, 0)
    full[me, :, :, 0:sets] = acc[:, 0:sets].astype(jnp.bfloat16).reshape(planes, width, sets)
    basis = acc[:, sets : sets + nb] + acc[:, sets + nb : sets + 2 * nb]
    high = basis.astype(jnp.bfloat16)
    low = (basis - high.astype(jnp.float32)).astype(jnp.bfloat16)
    full[me, :, :, sets : sets + 2 * nb] = jnp.concatenate([high, low], axis=1).reshape(
        planes, width, 2 * nb
    )

    core = lax.rem(me, 2)
    x, y = lax.rem(me // 2, 4), me // 8
    ia, ib = x + core * (y - x), y + core * (x - y)

    def pid(i, j):
        return lax.rem(i, 4) * (2 + 6 * core) + lax.rem(j, 4) * (8 - 6 * core) + core

    next_a, last_a = pid(ia + 1, ib), pid(ia + 3, ib)
    next_b, last_b = pid(ia, ib + 1), pid(ia, ib + 3)
    partner = me + 1 - 2 * core
    sent = []

    def piece(q, h):
        return full.at[q, pl.ds(h * (planes // 2), planes // 2)]

    def give(q, h, to):
        copy = push(
            piece(q, h), piece(q, h), g_send.at[len(sent)], g_recv.at[q * 2 + h], {"path": to}
        )
        copy.start()
        sent.append(copy)

    def take(q, h):
        push(
            piece(q, h), piece(q, h), g_send.at[0], g_recv.at[q * 2 + h], {"path": partner}
        ).wait_recv()

    for h in range(2):
        give(me, h, next_a)
        give(me, h, last_a)
        give(me, h, next_b)
        give(me, h, last_b)
    for h in range(2):
        give(me, h, partner)
    q1, q2, q3 = pid(ia + 3, ib), pid(ia + 1, ib), pid(ia + 2, ib)
    take(q1, 0)
    give(q1, 0, next_a)
    take(q2, 0)
    take(q1, 1)
    take(q2, 1)
    give(q2, 1, last_a)
    for q in (q1, q2):
        for h in range(2):
            give(q, h, next_b)
            give(q, h, last_b)
            give(q, h, partner)
    for h in range(2):
        take(q3, h)
        give(q3, h, next_b)
        give(q3, h, last_b)
        give(q3, h, partner)

    shock_step(2)

    for i in (ia, ia + 3, ia + 1, ia + 2):
        r1, r2 = pid(i, ib + 3), pid(i, ib + 1)
        take(r1, 0)
        give(r1, 0, next_b)
        take(r2, 0)
        take(r1, 1)
        take(r2, 1)
        give(r2, 1, last_b)
        for r in (r1, r2):
            for h in range(2):
                give(r, h, partner)

    shock_step(3)

    for i in (ia, ia + 3, ia + 1, ia + 2):
        r3 = pid(i, ib + 2)
        for h in range(2):
            take(r3, h)
            give(r3, h, partner)

    @pl.loop(0, group // 2)
    def _(q):
        for h in range(2):
            take(2 * q + 1 - core, h)

    shock_up(up_source(4), 0).wait_recv()
    shock_down(down_source(4), 1).wait_recv()

    acc2 = acc
    acc2[...] = jnp.zeros_like(acc2)

    def drive(n, _):
        source = lax.rem(
            z + planes + jnp.where(lax.rem(n, 2) == 1, -((n + 1) // 2), n // 2), planes
        )
        left = shocks[source].reshape(2 * half_rows, cols)
        right = full[:, source].reshape(cols, full.shape[3])
        acc2[...] += jnp.dot(left, right, preferred_element_type=jnp.float32)
        return 0

    lax.fori_loop(0, planes, drive, 0)
    drive_ref[...] = acc2[:, 0:sets]
    proj_ref[...] = acc2[:, sets : sets + nb] + acc2[:, sets + nb : sets + 2 * nb]

    for copy in sent:
        copy.wait_send()
    for k in range(0, 4):
        for h in range(2):
            if k < 3 or h == 0:
                shock_up(up_source(k), h).wait_send()
            if k < 3 or h == 1:
                shock_down(down_source(k), h).wait_send()

    @pl.loop(1, planes)
    def _(d):
        vol_copy(d).wait_send()

    @pl.when(me >= per_plane * z)
    def _():
        @pl.loop(1, group)
        def _(d):
            slice_copy(d).wait_send()

    @pl.loop(0, 5)
    def _(k):
        low, high = up_source(k), down_source(k)
        rise, fall = rises(low), planes - 1 - rises(high)

        @pl.loop(0, planes)
        def _(g):
            @pl.when((g >= low) & (k < rise))
            def _():
                slice_up(low, g).wait_send()

            @pl.when((g >= high) & (k < fall))
            def _():
                slice_down(high, g).wait_send()


def front(shocks, chol_factor, factor_vol, trade_loading, basis_loading, steps):
    planes, group = lax.axis_size("fac"), lax.axis_size("path")
    rows, cols = shocks.shape
    height = chol_factor.shape[0]
    width = cols // group
    total, sets = trade_loading.shape
    nb = basis_loading.shape[1]
    wide = sets + 2 * nb
    vmem = pl.BlockSpec(memory_space=pltpu.VMEM)
    hbm = pl.BlockSpec(memory_space=pl.ANY)
    dma = pltpu.SemaphoreType.DMA
    return pl.pallas_call(
        functools.partial(front_kernel, planes, group, 1.0 / math.sqrt(steps)),
        out_shape=(
            jax.ShapeDtypeStruct((rows, sets), jnp.float32),
            jax.ShapeDtypeStruct((rows, nb), jnp.float32),
        ),
        in_specs=[vmem, hbm, vmem, hbm, vmem],
        out_specs=(vmem, vmem),
        scratch_shapes=[
            pltpu.VMEM((group, width, height), jnp.bfloat16),
            pltpu.VMEM((group, planes, width, height), jnp.bfloat16),
            pltpu.VMEM((planes, 2, rows // 2, cols), jnp.bfloat16),
            pltpu.VMEM((planes, cols // 128, 128), jnp.float32),
            pltpu.VMEM((total, wide), jnp.bfloat16),
            pltpu.VMEM((group, planes, width, wide), jnp.bfloat16),
            pltpu.VMEM((rows, wide), jnp.float32),
            dma((3,)),
            dma((group,)),
            dma((group,)),
            dma((planes,)),
            dma((planes,)),
            dma((2 * planes,)),
            dma((2 * planes,)),
            dma((2 * planes,)),
            dma((planes * planes,)),
            dma((planes * planes,)),
            dma((planes * planes,)),
            dma((64,)),
            dma((2 * group,)),
        ],
        compiler_params=pltpu.CompilerParams(
            collective_id=0, has_side_effects=True, vmem_limit_bytes=62 * 2**20
        ),
    )(chol_factor, shocks, factor_vol, trade_loading, basis_loading)


def on_device(shocks, chol_factor, factor_vol, trade_loading, basis_loading, trade_set):
    step_count, path_count, fac_width = shocks.shape
    row_count = step_count * path_count
    sets_here = NSETS // lax.axis_size("fac")
    local_set = trade_set % sets_here
    member = (local_set[:, None] == jnp.arange(sets_here, dtype=jnp.int32)[None, :]).astype(
        jnp.bfloat16
    )
    drive, proj = front(
        shocks.reshape(row_count, fac_width),
        chol_factor,
        factor_vol.reshape(-1, 128),
        trade_loading,
        basis_loading,
        step_count,
    )
    drive = drive.reshape(step_count, path_count, -1)
    proj = proj.reshape(step_count, path_count, -1)
    return tail(drive, proj, member, path_count * lax.axis_size("path"))


def solution(mesh):
    in_specs = (P(None, "path", "fac"), P("path", "fac"), P("fac"), P(None, "fac"), P(), P("fac"))
    out_specs = P(None, "path", "fac")
    return jax.shard_map(
        on_device, mesh=mesh, in_specs=in_specs, out_specs=out_specs, check_vma=False
    )
```

```python
import functools
import math

import jax
import jax.numpy as jnp
from jax import lax
from jax.experimental import pallas as pl
from jax.experimental.pallas import tpu as pltpu
from jax.sharding import PartitionSpec as P

NSETS = 4096
MESH = pl.DeviceIdType.MESH
HIGH = lax.Precision.HIGHEST


def split_dot(a, b):
    high = a.astype(jnp.bfloat16)
    low = (a - high.astype(jnp.float32)).astype(jnp.bfloat16)
    both = jnp.dot(
        jnp.concatenate([high, low], axis=0), b, preferred_element_type=jnp.float32
    )
    rows = a.shape[0]
    return both[:rows] + both[rows:]


def invert(mats):
    n = mats[0].shape[0]
    count = len(mats)
    row = lax.broadcasted_iota(jnp.int32, (n, 2 * n), 0)
    lane = lax.broadcasted_iota(jnp.int32, (n, 2 * n), 1)
    eye = jnp.where(lane == row + n, 1.0, 0.0)
    wide = [jnp.concatenate([m, jnp.zeros_like(m)], axis=1) + eye for m in mats]
    blocks = tuple(tuple(w[8 * b : 8 * b + 8] for b in range(n // 8)) for w in wide)
    sub = lax.broadcasted_iota(jnp.int32, (8, 1), 0)

    def body(_, blocks):
        done = []
        for m in range(count):
            rows = list(blocks[m])
            for k in range(8):
                pivot_row = rows[0][k : k + 1, :]
                inverse = 1.0 / pivot_row[:, k : k + 1]
                scaled = pivot_row * inverse
                fresh = []
                for b in range(n // 8):
                    col = rows[b][:, k : k + 1]
                    if b == 0:
                        col = jnp.where(sub == k, col - 1.0, col)
                    fresh.append(rows[b] - col * scaled)
                rows = fresh
            rows = rows[1:] + rows[:1]
            done.append(tuple(pltpu.roll(r, 2 * n - 8, 1) for r in rows))
        return tuple(done)

    blocks = lax.fori_loop(0, n // 8, body, blocks)
    return [jnp.concatenate(b, axis=0)[:, :n] for b in blocks]


def push(src, dst, send_sem, recv_sem, where):
    return pltpu.make_async_remote_copy(
        src_ref=src, dst_ref=dst, send_sem=send_sem, recv_sem=recv_sem,
        device_id=where, device_id_type=MESH,
    )


def rises(s):
    extra = [0, 1, 3, 3, 0, 1, 1, 0]
    total = 2
    for at, more in enumerate(extra):
        if more:
            total = total + jnp.where(s == at, more, 0)
    return total


def kernel(
    planes, group, scale, total_paths,
    chol_ref, shock_hbm, vol_ref, trade_hbm, basis_ref, member_ref, out_ref,
    turned, slices, shocks, vols, loads, full, acc,
    gram_part, gram_in, gram_sum, part, landed, total, base,
    local_sem, a_send, a_recv, v_send, v_recv, s_up, s_down, s_recv,
    c_up, c_down, c_recv, g_send, g_recv, t_send, t_recv,
):
    me = lax.axis_index("path")
    z = lax.axis_index("fac")
    above, below = {"fac": lax.rem(z + 1, planes)}, {"fac": lax.rem(z + planes - 1, planes)}
    per_plane = group // planes
    height, cols = chol_ref.shape
    width = cols // group
    sets = trade_hbm.shape[1]
    nb = basis_ref.shape[0]
    half_rows = shock_hbm.shape[0] // 2
    steps, paths = out_ref.shape[0:2]

    barrier = pltpu.get_barrier_semaphore()

    @pl.loop(1, group)
    def _(d):
        pl.semaphore_signal(
            barrier, inc=1, device_id={"path": lax.rem(me + d, group)}, device_id_type=MESH
        )

    @pl.loop(1, planes)
    def _(d):
        pl.semaphore_signal(
            barrier, inc=1, device_id={"fac": lax.rem(z + d, planes)}, device_id_type=MESH
        )

    load_shocks = [
        pltpu.make_async_copy(
            shock_hbm.at[pl.ds(h * half_rows, half_rows)], shocks.at[z, h], local_sem.at[1 + h]
        )
        for h in range(2)
    ]
    for copy in load_shocks:
        copy.start()
    load_trades = pltpu.make_async_copy(trade_hbm, loads.at[:, 0:sets], local_sem.at[0])
    load_trades.start()

    for b in range(cols // 128):
        block = chol_ref[:, 128 * b : 128 * (b + 1)].T
        at = pl.ds(b * (128 // width), 128 // width)
        turned[at] = block.reshape(128 // width, width, height)
    vols[z] = vol_ref[...]
    for g in range(planes - 1):
        slices[g * per_plane : (g + 1) * per_plane, g + 1 : planes] = jnp.zeros(
            (per_plane, planes - 1 - g, width, height), jnp.bfloat16
        )
    for copy in load_shocks:
        copy.wait()

    pl.semaphore_wait(barrier, group - 1 + planes - 1)

    def up_source(k):
        return lax.rem(z + planes - k, planes)

    def down_source(k):
        return lax.rem(z + k, planes)

    def slice_copy(d):
        to = lax.rem(me + d, group)
        return push(turned.at[to], slices.at[me, z], a_send.at[to], a_recv.at[me], {"path": to})

    def slice_taken(source):
        return push(
            turned.at[source], slices.at[source, z], a_send.at[source], a_recv.at[source],
            {"path": source},
        )

    @pl.when(me >= per_plane * z)
    def _():
        @pl.loop(1, group)
        def _(d):
            slice_copy(d).start()

        slices[me, z] = turned[me]

    def shock_up(s, h):
        return push(shocks.at[s, h], shocks.at[s, h], s_up.at[s * 2 + h], s_recv.at[s * 2 + h], above)

    def shock_down(s, h):
        return push(
            shocks.at[s, h], shocks.at[s, h], s_down.at[s * 2 + h], s_recv.at[s * 2 + h], below
        )

    def vol_copy(d):
        to = lax.rem(z + d, planes)
        return push(vols.at[z], vols.at[z], v_send.at[to], v_recv.at[z], {"fac": to})

    def vol_taken(d):
        source = lax.rem(z + d, planes)
        return push(
            vols.at[source], vols.at[source], v_send.at[source], v_recv.at[source], {"fac": source}
        )

    @pl.loop(1, planes)
    def _(d):
        vol_copy(d).start()

    shock_up(z, 0).start()
    shock_down(z, 0).start()

    @pl.loop(1, group)
    def _(d):
        source = lax.rem(me + d, group)

        @pl.when(source >= per_plane * z)
        def _():
            slice_taken(source).wait_recv()

    def block(s, g):
        return slices.at[pl.ds(g * per_plane, per_plane), s]

    def slice_up(s, g):
        return push(
            block(s, g), block(s, g), c_up.at[s * planes + g], c_recv.at[s * planes + g], above
        )

    def slice_down(s, g):
        return push(
            block(s, g), block(s, g), c_down.at[s * planes + g], c_recv.at[s * planes + g], below
        )

    @pl.loop(0, planes)
    def _(g):
        @pl.when(g >= z)
        def _():
            slice_up(z, g).start()
            slice_down(z, g).start()

    shock_up(z, 1).start()
    shock_down(z, 1).start()

    @pl.loop(1, planes)
    def _(d):
        vol_taken(d).wait_recv()

    load_trades.wait()
    vol_rows = vols[...].reshape(planes * vol_ref.shape[0], 128) * scale
    vol_rows = jnp.concatenate(
        [vol_rows, jnp.zeros((128 - vol_rows.shape[0], 128), jnp.float32)], axis=0
    )

    def scale_rows(c, columns):
        column = columns[:, 0:1]
        at = pl.ds(pl.multiple_of(c * 128, 128), 128)
        loads[at, 0:sets] = (loads[at, 0:sets].astype(jnp.float32) * column).astype(jnp.bfloat16)
        basis = basis_ref[:, at].astype(jnp.float32).T * column
        high = basis.astype(jnp.bfloat16)
        low = (basis - high.astype(jnp.float32)).astype(jnp.bfloat16)
        loads[at, sets : sets + 2 * nb] = jnp.concatenate([high, low], axis=1)
        return pltpu.roll(columns, 127, 1)

    lax.fori_loop(0, loads.shape[0] // 128, scale_rows, vol_rows.T)

    def slice_step(k):
        low, high = up_source(k), down_source(k)
        rise, fall = rises(low), planes - 1 - rises(high)

        @pl.loop(0, planes)
        def _(g):
            @pl.when((g >= low) & (k <= rise))
            def _():
                slice_up(low, g).wait_recv()

                @pl.when(k < rise)
                def _():
                    slice_up(low, g).start()

            @pl.when((g >= high) & (k <= fall))
            def _():
                slice_down(high, g).wait_recv()

                @pl.when(k < fall)
                def _():
                    slice_down(high, g).start()

    def shock_step(k):
        for h in range(2):
            shock_up(up_source(k), h).wait_recv()
            shock_down(down_source(k), h).wait_recv()
            if k < 3 or h == 0:
                shock_up(up_source(k), h).start()
            if k < 3 or h == 1:
                shock_down(down_source(k), h).start()

    offsets = [0, -1, 1, -2, 2, -3, 3, 4]

    def plane_at(n):
        return lax.rem(z + planes + offsets[n], planes)

    waves = [(0, 5), (5, 8)]
    cuts = [(0, 3), (3, 5), (5, 6), (6, 8)]

    def make(first, last):
        count = (last - first) * width
        acc[0:count] = jnp.zeros((count, acc.shape[1]), jnp.float32)

        def add(q, _):
            left = jnp.concatenate(
                [slices[q, plane_at(n)] for n in range(first, last)], axis=0
            )
            at = pl.ds(pl.multiple_of(q * height, height), height)
            acc[0:count] += jnp.dot(left, loads[at, :], preferred_element_type=jnp.float32)
            return 0

        lax.fori_loop(0, group, add, 0)
        full[me, first:last, :, 0:sets] = (
            acc[0:count, 0:sets].astype(jnp.bfloat16).reshape(last - first, width, sets)
        )
        basis = acc[0:count, sets : sets + nb] + acc[0:count, sets + nb : sets + 2 * nb]
        high = basis.astype(jnp.bfloat16)
        low = (basis - high.astype(jnp.float32)).astype(jnp.bfloat16)
        full[me, first:last, :, sets : sets + 2 * nb] = jnp.concatenate(
            [high, low], axis=1
        ).reshape(last - first, width, 2 * nb)

    core = lax.rem(me, 2)
    x, y = lax.rem(me // 2, 4), me // 8
    ia, ib = x + core * (y - x), y + core * (x - y)

    def pid(i, j):
        return lax.rem(i, 4) * (2 + 6 * core) + lax.rem(j, 4) * (8 - 6 * core) + core

    next_a, last_a = pid(ia + 1, ib), pid(ia + 3, ib)
    next_b, last_b = pid(ia, ib + 1), pid(ia, ib + 3)
    partner = me + 1 - 2 * core
    q1, q2, q3 = pid(ia + 3, ib), pid(ia + 1, ib), pid(ia + 2, ib)
    sent = []

    def piece(q, cut):
        first, last = cuts[cut]
        return full.at[q, pl.ds(first, last - first)]

    def give(q, cut, to):
        copy = push(
            piece(q, cut), piece(q, cut), g_send.at[len(sent)], g_recv.at[q * 4 + cut], {"path": to}
        )
        copy.start()
        sent.append(copy)

    def take(q, cut):
        push(
            piece(q, cut), piece(q, cut), g_send.at[0], g_recv.at[q * 4 + cut], {"path": partner}
        ).wait_recv()

    def gather_own(w):
        for cut in (2 * w, 2 * w + 1):
            give(me, cut, next_a)
            give(me, cut, last_a)
            give(me, cut, next_b)
            give(me, cut, last_b)
        for cut in (2 * w, 2 * w + 1):
            give(me, cut, partner)

    def gather_first(w):
        up, down = 2 * w, 2 * w + 1
        take(q1, up)
        give(q1, up, next_a)
        take(q2, down)
        give(q2, down, last_a)
        take(q1, down)
        take(q2, up)
        for q in (q1, q2):
            for cut in (up, down):
                give(q, cut, next_b)
                give(q, cut, last_b)
                give(q, cut, partner)
        for cut in (up, down):
            take(q3, cut)
            give(q3, cut, next_b)
            give(q3, cut, last_b)
            give(q3, cut, partner)

    def gather_second(w):
        up, down = 2 * w, 2 * w + 1
        for i in (ia, ia + 3, ia + 1, ia + 2):
            r1, r2 = pid(i, ib + 3), pid(i, ib + 1)
            take(r1, up)
            give(r1, up, next_b)
            take(r2, down)
            give(r2, down, last_b)
            take(r1, down)
            take(r2, up)
            for r in (r1, r2):
                for cut in (up, down):
                    give(r, cut, partner)

    def gather_last(w):
        for i in (ia, ia + 3, ia + 1, ia + 2):
            r3 = pid(i, ib + 2)
            for cut in (2 * w, 2 * w + 1):
                take(r3, cut)
                give(r3, cut, partner)

    def gather_partner(w):
        @pl.loop(0, group // 2)
        def _(q):
            for cut in (2 * w, 2 * w + 1):
                take(2 * q + 1 - core, cut)

    slice_step(1)
    slice_step(2)
    make(*waves[0])
    gather_own(0)
    slice_step(3)
    gather_first(0)
    slice_step(4)
    shock_step(1)
    gather_second(0)
    slice_step(5)
    make(*waves[1])
    gather_own(1)
    gather_last(0)
    gather_first(1)
    shock_step(2)
    gather_second(1)
    gather_partner(0)
    shock_step(3)

    acc[...] = jnp.zeros_like(acc)

    def drive(first, last):
        for n in range(first, last):
            left = shocks[plane_at(n)].reshape(2 * half_rows, cols)
            right = full[:, n].reshape(cols, full.shape[3])
            acc[...] += jnp.dot(left, right, preferred_element_type=jnp.float32)

    drive(0, 5)
    gather_last(1)
    gather_partner(1)
    shock_up(up_source(4), 0).wait_recv()
    shock_down(down_source(4), 1).wait_recv()
    drive(5, 8)

    def scatter(src, dst, lane, d):
        to = lax.rem(me + d, group)
        return push(
            src.at[to], dst.at[me], t_send.at[lane * group + to], t_recv.at[lane * group + me],
            {"path": to},
        )

    def share(src, lane, d):
        to = lax.rem(me + d, group)
        return push(
            src.at[me], src.at[me], t_send.at[lane * group + to], t_recv.at[lane * group + me],
            {"path": to},
        )

    def taken(dst, lane, d):
        source = lax.rem(me + d, group)
        return push(
            dst.at[source], dst.at[source], t_send.at[lane * group + source],
            t_recv.at[lane * group + source], {"path": source},
        )

    def each(action):
        @pl.loop(1, group)
        def _(d):
            action(d)

    contract = (((0,), (0,)), ((), ()))
    rows = nb // 8
    w = jnp.zeros((paths, nb), jnp.float32)
    for t in range(steps):
        here = pl.ds(t * paths, paths)
        w = w + (acc[here, sets : sets + nb] + acc[here, sets + nb : sets + 2 * nb])
        basis = jnp.tanh(w)
        base[t] = basis
        gram = lax.dot_general(
            basis, basis, contract, precision=HIGH, preferred_element_type=jnp.float32
        )
        gram = jnp.concatenate([gram, jnp.zeros_like(gram)], axis=1)
        gram_part[t * rows : (t + 1) * rows] = gram.reshape(rows, 8, 2 * nb)
    each(lambda d: scatter(gram_part, gram_in, 0, d).start())
    gram_in[me] = gram_part[me]

    v = jnp.zeros((paths, sets), jnp.float32)
    for t in range(steps):
        v = v + acc[pl.ds(t * paths, paths), 0:sets]
        values = jnp.maximum(v, 0.0) + jnp.log(1.0 + jnp.exp(-jnp.abs(v))) - 1.0
        moment = lax.dot_general(
            base[t], values, contract, precision=HIGH, preferred_element_type=jnp.float32
        )
        part[t * rows : (t + 1) * rows] = moment.reshape(rows, 8, sets)
    each(lambda d: scatter(part, landed, 1, d).start())
    landed[me] = part[me]

    each(lambda d: taken(gram_in, 0, d).wait_recv())
    gram_sum[me] = jnp.sum(gram_in[...], axis=0)
    each(lambda d: share(gram_sum, 2, d).start())

    each(lambda d: taken(landed, 1, d).wait_recv())
    total[me] = split_dot(jnp.sum(landed[...], axis=0), member_ref[...])
    each(lambda d: share(total, 3, d).start())

    each(lambda d: taken(gram_sum, 2, d).wait_recv())
    row = lax.broadcasted_iota(jnp.int32, (nb, nb), 0)
    lane = lax.broadcasted_iota(jnp.int32, (nb, nb), 1)
    ridge = jnp.where(row == lane, 0.01 * total_paths, 0.0)
    inverses = invert(
        [
            gram_sum[t * rows : (t + 1) * rows, :, 0:nb].reshape(nb, nb) + ridge
            for t in range(steps)
        ]
    )
    weights = [
        jnp.dot(base[t], inverses[t], precision=HIGH, preferred_element_type=jnp.float32)
        for t in range(steps)
    ]
    each(lambda d: taken(total, 3, d).wait_recv())
    for t in range(steps):
        moment = total[t * rows : (t + 1) * rows].reshape(nb, sets)
        predicted = jnp.dot(
            weights[t], moment, precision=HIGH, preferred_element_type=jnp.float32
        )
        out_ref[t] = jnp.maximum(predicted, 0.0)

    each(lambda d: scatter(gram_part, gram_in, 0, d).wait_send())
    each(lambda d: scatter(part, landed, 1, d).wait_send())
    each(lambda d: share(gram_sum, 2, d).wait_send())
    each(lambda d: share(total, 3, d).wait_send())
    for copy in sent:
        copy.wait_send()
    for k in range(0, 4):
        for h in range(2):
            if k < 3 or h == 0:
                shock_up(up_source(k), h).wait_send()
            if k < 3 or h == 1:
                shock_down(down_source(k), h).wait_send()

    @pl.loop(1, planes)
    def _(d):
        vol_copy(d).wait_send()

    @pl.when(me >= per_plane * z)
    def _():
        each(lambda d: slice_copy(d).wait_send())

    @pl.loop(0, 5)
    def _(k):
        low, high = up_source(k), down_source(k)
        rise, fall = rises(low), planes - 1 - rises(high)

        @pl.loop(0, planes)
        def _(g):
            @pl.when((g >= low) & (k < rise))
            def _():
                slice_up(low, g).wait_send()

            @pl.when((g >= high) & (k < fall))
            def _():
                slice_down(high, g).wait_send()


def on_device(shocks, chol_factor, factor_vol, trade_loading, basis_loading, trade_set):
    steps, paths, cols = shocks.shape
    planes, group = lax.axis_size("fac"), lax.axis_size("path")
    rows = steps * paths
    height = chol_factor.shape[0]
    width = cols // group
    total, sets = trade_loading.shape
    nb = basis_loading.shape[1]
    wide = sets + 2 * nb
    local_set = trade_set % (NSETS // planes)
    member = (local_set[:, None] == jnp.arange(sets, dtype=jnp.int32)[None, :]).astype(
        jnp.bfloat16
    )
    vmem = pl.BlockSpec(memory_space=pltpu.VMEM)
    hbm = pl.BlockSpec(memory_space=pl.ANY)
    dma = pltpu.SemaphoreType.DMA
    return pl.pallas_call(
        functools.partial(
            kernel, planes, group, 1.0 / math.sqrt(steps), paths * group
        ),
        out_shape=jax.ShapeDtypeStruct((steps, paths, sets), jnp.float32),
        in_specs=[vmem, hbm, vmem, hbm, vmem, vmem],
        out_specs=vmem,
        scratch_shapes=[
            pltpu.VMEM((group, width, height), jnp.bfloat16),
            pltpu.VMEM((group, planes, width, height), jnp.bfloat16),
            pltpu.VMEM((planes, 2, rows // 2, cols), jnp.bfloat16),
            pltpu.VMEM((planes, cols // 128, 128), jnp.float32),
            pltpu.VMEM((total, wide), jnp.bfloat16),
            pltpu.VMEM((group, planes, width, wide), jnp.bfloat16),
            pltpu.VMEM((rows, wide), jnp.float32),
            pltpu.VMEM((group, 8, 2 * nb), jnp.float32),
            pltpu.VMEM((group, 8, 2 * nb), jnp.float32),
            pltpu.VMEM((group, 8, 2 * nb), jnp.float32),
            pltpu.VMEM((group, 8, sets), jnp.float32),
            pltpu.VMEM((group, 8, sets), jnp.float32),
            pltpu.VMEM((group, 8, sets), jnp.float32),
            pltpu.VMEM((steps, paths, nb), jnp.float32),
            dma((3,)),
            dma((group,)),
            dma((group,)),
            dma((planes,)),
            dma((planes,)),
            dma((2 * planes,)),
            dma((2 * planes,)),
            dma((2 * planes,)),
            dma((planes * planes,)),
            dma((planes * planes,)),
            dma((planes * planes,)),
            dma((128,)),
            dma((4 * group,)),
            dma((4 * group,)),
            dma((4 * group,)),
        ],
        compiler_params=pltpu.CompilerParams(
            collective_id=0, has_side_effects=True, vmem_limit_bytes=62 * 2**20
        ),
    )(
        chol_factor,
        shocks.reshape(rows, cols),
        factor_vol.reshape(-1, 128),
        trade_loading,
        basis_loading.T,
        member,
    )


def solution(mesh):
    in_specs = (P(None, "path", "fac"), P("path", "fac"), P("fac"), P(None, "fac"), P(), P("fac"))
    out_specs = P(None, "path", "fac")
    return jax.shard_map(
        on_device, mesh=mesh, in_specs=in_specs, out_specs=out_specs, check_vma=False
    )
```

```python
import functools
import math

import jax
import jax.numpy as jnp
from jax import lax
from jax.experimental import pallas as pl
from jax.experimental.pallas import tpu as pltpu
from jax.sharding import PartitionSpec as P

MESH = pl.DeviceIdType.MESH
HIGH = lax.Precision.HIGHEST


def split_dot(a, b):
    high = a.astype(jnp.bfloat16)
    low = (a - high.astype(jnp.float32)).astype(jnp.bfloat16)
    both = lax.dot_general(
        jnp.concatenate([high, low], axis=0),
        b,
        (((1,), (1,)), ((), ())),
        preferred_element_type=jnp.float32,
    )
    rows = a.shape[0]
    return both[:rows] + both[rows:]


def invert(mats):
    n = mats[0].shape[0]
    count = len(mats)
    row = lax.broadcasted_iota(jnp.int32, (n, 2 * n), 0)
    lane = lax.broadcasted_iota(jnp.int32, (n, 2 * n), 1)
    eye = jnp.where(lane == row + n, 1.0, 0.0)
    wide = [jnp.concatenate([m, jnp.zeros_like(m)], axis=1) + eye for m in mats]
    blocks = tuple(tuple(w[8 * b : 8 * b + 8] for b in range(n // 8)) for w in wide)
    sub = lax.broadcasted_iota(jnp.int32, (8, 1), 0)

    def body(_, blocks):
        done = []
        for m in range(count):
            rows = list(blocks[m])
            for k in range(8):
                pivot_row = rows[0][k : k + 1, :]
                inverse = 1.0 / pivot_row[:, k : k + 1]
                scaled = pivot_row * inverse
                fresh = []
                for b in range(n // 8):
                    col = rows[b][:, k : k + 1]
                    if b == 0:
                        col = jnp.where(sub == k, col - 1.0, col)
                    fresh.append(rows[b] - col * scaled)
                rows = fresh
            rows = rows[1:] + rows[:1]
            done.append(tuple(pltpu.roll(r, 2 * n - 8, 1) for r in rows))
        return tuple(done)

    blocks = lax.fori_loop(0, n // 8, body, blocks)
    return [jnp.concatenate(b, axis=0)[:, :n] for b in blocks]


def push(src, dst, send_sem, recv_sem, where):
    return pltpu.make_async_remote_copy(
        src_ref=src, dst_ref=dst, send_sem=send_sem, recv_sem=recv_sem,
        device_id=where, device_id_type=MESH,
    )


def rises(s):
    return 3 + jnp.where((s >= 2) & (s <= 4), 1, 0)


def kernel(
    planes, group, scale, total_paths,
    chol_hbm, shock_hbm, vol_ref, trade_hbm, basis_hbm, set_ref, out_ref,
    chol_ref, basis_ref,
    turned, slices, shocks, vols, loads, full, acc,
    gram_part, gram_in, gram_sum, part, landed, total, base,
    local_sem, a_send, a_recv, v_send, v_recv, s_up, s_down, s_recv,
    c_up, c_down, c_recv, g_send, g_recv, t_send, t_recv,
):
    me = lax.axis_index("path")
    z = lax.axis_index("fac")
    above, below = {"fac": lax.rem(z + 1, planes)}, {"fac": lax.rem(z + planes - 1, planes)}
    per_plane = group // planes
    height, cols = chol_ref.shape
    width = cols // group
    sets = trade_hbm.shape[1]
    nb = basis_ref.shape[0]
    half_rows = shock_hbm.shape[0] // 2
    steps, paths = out_ref.shape[0:2]

    barrier = pltpu.get_barrier_semaphore()

    @pl.loop(1, group)
    def _(d):
        pl.semaphore_signal(
            barrier, inc=1, device_id={"path": lax.rem(me + d, group)}, device_id_type=MESH
        )

    @pl.loop(1, planes)
    def _(d):
        pl.semaphore_signal(
            barrier, inc=1, device_id={"fac": lax.rem(z + d, planes)}, device_id_type=MESH
        )

    load_shocks = [
        pltpu.make_async_copy(
            shock_hbm.at[pl.ds(h * half_rows, half_rows)], shocks.at[z, h], local_sem.at[1 + h]
        )
        for h in range(2)
    ]
    for copy in load_shocks:
        copy.start()
    load_chol = pltpu.make_async_copy(chol_hbm, chol_ref, local_sem.at[3])
    load_chol.start()
    load_basis = pltpu.make_async_copy(basis_hbm, basis_ref, local_sem.at[4])
    load_basis.start()
    load_trades = pltpu.make_async_copy(trade_hbm, loads.at[:, 0:sets], local_sem.at[0])
    load_trades.start()
    load_chol.wait()

    for b in range(cols // 128):
        block = chol_ref[:, 128 * b : 128 * (b + 1)].T
        at = pl.ds(b * (128 // width), 128 // width)
        turned[at] = block.reshape(128 // width, width, height)
    vols[z] = vol_ref[...]
    for g in range(planes - 1):
        slices[g * per_plane : (g + 1) * per_plane, g + 1 : planes] = jnp.zeros(
            (per_plane, planes - 1 - g, width, height), jnp.bfloat16
        )
    for copy in load_shocks:
        copy.wait()

    pl.semaphore_wait(barrier, group - 1 + planes - 1)

    def up_source(k):
        return lax.rem(z + planes - k, planes)

    def down_source(k):
        return lax.rem(z + k, planes)

    def slice_copy(d):
        to = lax.rem(me + d, group)
        return push(turned.at[to], slices.at[me, z], a_send.at[to], a_recv.at[me], {"path": to})

    def slice_taken(source):
        return push(
            turned.at[source], slices.at[source, z], a_send.at[source], a_recv.at[source],
            {"path": source},
        )

    @pl.when(me >= per_plane * z)
    def _():
        @pl.loop(1, group)
        def _(d):
            slice_copy(d).start()

        slices[me, z] = turned[me]

    def shock_up(s, h):
        return push(shocks.at[s, h], shocks.at[s, h], s_up.at[s * 2 + h], s_recv.at[s * 2 + h], above)

    def shock_down(s, h):
        return push(
            shocks.at[s, h], shocks.at[s, h], s_down.at[s * 2 + h], s_recv.at[s * 2 + h], below
        )

    def vol_copy(d):
        to = lax.rem(z + d, planes)
        return push(vols.at[z], vols.at[z], v_send.at[to], v_recv.at[z], {"fac": to})

    def vol_taken(d):
        source = lax.rem(z + d, planes)
        return push(
            vols.at[source], vols.at[source], v_send.at[source], v_recv.at[source], {"fac": source}
        )

    @pl.loop(1, planes)
    def _(d):
        vol_copy(d).start()

    shock_up(z, 0).start()
    shock_down(z, 0).start()

    @pl.loop(1, group)
    def _(d):
        source = lax.rem(me + d, group)

        @pl.when(source >= per_plane * z)
        def _():
            slice_taken(source).wait_recv()

    def block(s, g):
        return slices.at[pl.ds(g * per_plane, per_plane), s]

    def slice_up(s, g):
        return push(
            block(s, g), block(s, g), c_up.at[s * planes + g], c_recv.at[s * planes + g], above
        )

    def slice_down(s, g):
        return push(
            block(s, g), block(s, g), c_down.at[s * planes + g], c_recv.at[s * planes + g], below
        )

    @pl.loop(0, planes)
    def _(g):
        @pl.when(g >= z)
        def _():
            slice_up(z, g).start()
            slice_down(z, g).start()

    @pl.loop(1, planes)
    def _(d):
        vol_taken(d).wait_recv()

    load_trades.wait()
    load_basis.wait()
    vol_rows = vols[...].reshape(planes * vol_ref.shape[0], 128) * scale
    vol_rows = jnp.concatenate(
        [vol_rows, jnp.zeros((128 - vol_rows.shape[0], 128), jnp.float32)], axis=0
    )

    def scale_rows(c, columns):
        column = columns[:, 0:1]
        at = pl.ds(pl.multiple_of(c * 128, 128), 128)
        loads[at, 0:sets] = (loads[at, 0:sets].astype(jnp.float32) * column).astype(jnp.bfloat16)
        basis = basis_ref[:, at].astype(jnp.float32).T * column
        high = basis.astype(jnp.bfloat16)
        low = (basis - high.astype(jnp.float32)).astype(jnp.bfloat16)
        loads[at, sets : sets + 2 * nb] = jnp.concatenate([high, low], axis=1)
        return pltpu.roll(columns, 127, 1)

    def slice_unit(k, g):
        low, high = up_source(k), down_source(k)
        rise, fall = rises(low), planes - 1 - rises(high)

        @pl.when((g >= low) & (k <= rise))
        def _():
            slice_up(low, g).wait_recv()

            @pl.when(k < rise)
            def _():
                slice_up(low, g).start()

        @pl.when((g >= high) & (k <= fall))
        def _():
            slice_down(high, g).wait_recv()

            @pl.when(k < fall)
            def _():
                slice_down(high, g).start()

    def slice_step(k):
        @pl.loop(0, planes)
        def _(g):
            slice_unit(k, g)

    def shock_step(k, h):
        shock_up(up_source(k), h).wait_recv()
        shock_down(down_source(k), h).wait_recv()
        if k < 3 or h == 0:
            shock_up(up_source(k), h).start()
        if k < 3 or h == 1:
            shock_down(down_source(k), h).start()

    offsets = [0, -1, 1, -2, 2, -3, 3, 4]

    def plane_at(n):
        return lax.rem(z + planes + offsets[n], planes)

    waves = [(0, 5), (5, 8)]
    cuts = [(0, 3), (3, 5), (5, 6), (6, 8)]

    def make(first, last, k):
        count = (last - first) * width
        acc[0:count] = jnp.zeros((count, acc.shape[1]), jnp.float32)

        @pl.loop(0, planes)
        def _(g):
            left = jnp.concatenate(
                [
                    jnp.concatenate(
                        [slices[g * per_plane + r, plane_at(n)] for n in range(first, last)], axis=0
                    )
                    for r in range(per_plane)
                ],
                axis=1,
            )
            deep = height * per_plane
            at = pl.ds(pl.multiple_of(g * deep, deep), deep)
            acc[0:count] += jnp.dot(left, loads[at, :], preferred_element_type=jnp.float32)
            if k:
                slice_unit(k, g)

        full[me, first:last, :, 0:sets] = (
            acc[0:count, 0:sets].astype(jnp.bfloat16).reshape(last - first, width, sets)
        )
        basis = acc[0:count, sets : sets + nb] + acc[0:count, sets + nb : sets + 2 * nb]
        high = basis.astype(jnp.bfloat16)
        low = (basis - high.astype(jnp.float32)).astype(jnp.bfloat16)
        full[me, first:last, :, sets : sets + 2 * nb] = jnp.concatenate(
            [high, low], axis=1
        ).reshape(last - first, width, 2 * nb)

    core = lax.rem(me, 2)
    x, y = lax.rem(me // 2, 4), me // 8
    ia, ib = x + core * (y - x), y + core * (x - y)

    def pid(i, j):
        return lax.rem(i, 4) * (2 + 6 * core) + lax.rem(j, 4) * (8 - 6 * core) + core

    next_a, last_a = pid(ia + 1, ib), pid(ia + 3, ib)
    next_b, last_b = pid(ia, ib + 1), pid(ia, ib + 3)
    partner = me + 1 - 2 * core
    q1, q2, q3 = pid(ia + 3, ib), pid(ia + 1, ib), pid(ia + 2, ib)
    sent = []

    def piece(q, cut):
        first, last = cuts[cut]
        return full.at[q, pl.ds(first, last - first)]

    def give(q, cut, to):
        copy = push(
            piece(q, cut), piece(q, cut), g_send.at[len(sent)], g_recv.at[q * 4 + cut], {"path": to}
        )
        copy.start()
        sent.append(copy)

    def take(q, cut):
        push(
            piece(q, cut), piece(q, cut), g_send.at[0], g_recv.at[q * 4 + cut], {"path": partner}
        ).wait_recv()

    def gather_own(w):
        for cut in (2 * w, 2 * w + 1):
            give(me, cut, next_a)
            give(me, cut, last_a)
            give(me, cut, next_b)
            give(me, cut, last_b)
        for cut in (2 * w, 2 * w + 1):
            give(me, cut, partner)

    def gather_first(w):
        up, down = 2 * w, 2 * w + 1
        take(q1, up)
        give(q1, up, next_a)
        take(q2, down)
        give(q2, down, last_a)
        take(q1, down)
        take(q2, up)
        for q in (q1, q2):
            for cut in (up, down):
                give(q, cut, next_b)
                give(q, cut, last_b)
                give(q, cut, partner)
        for cut in (up, down):
            take(q3, cut)
            give(q3, cut, next_b)
            give(q3, cut, last_b)
            give(q3, cut, partner)

    def gather_second(w):
        up, down = 2 * w, 2 * w + 1
        for i in (ia, ia + 3, ia + 1, ia + 2):
            r1, r2 = pid(i, ib + 3), pid(i, ib + 1)
            take(r1, up)
            give(r1, up, next_b)
            take(r2, down)
            give(r2, down, last_b)
            take(r1, down)
            take(r2, up)
            for r in (r1, r2):
                for cut in (up, down):
                    give(r, cut, partner)

    def gather_last(w):
        for i in (ia, ia + 3, ia + 1, ia + 2):
            r3 = pid(i, ib + 2)
            for cut in (2 * w, 2 * w + 1):
                take(r3, cut)
                give(r3, cut, partner)

    def gather_partner(w):
        @pl.loop(0, group // 2)
        def _(q):
            for cut in (2 * w, 2 * w + 1):
                take(2 * q + 1 - core, cut)

    def scale_part(g, columns):
        columns = lax.fori_loop(g * per_part, (g + 1) * per_part, scale_rows, columns)
        slice_unit(1, g)
        return columns

    per_part = loads.shape[0] // 128 // planes
    lax.fori_loop(0, planes, scale_part, vol_rows.T)
    shock_up(z, 1).start()
    shock_down(z, 1).start()
    slice_step(2)
    shock_step(1, 0)
    make(*waves[0], 3)
    gather_own(0)
    shock_step(1, 1)
    slice_step(4)
    gather_first(0)
    shock_step(2, 0)
    make(*waves[1], 0)
    gather_own(1)
    gather_second(0)
    shock_step(2, 1)
    gather_first(1)
    gather_last(0)
    shock_step(3, 0)
    shock_step(3, 1)
    gather_second(1)
    gather_partner(0)

    acc[...] = jnp.zeros_like(acc)

    def drive(first, last):
        for n in range(first, last):
            left = shocks[plane_at(n)].reshape(2 * half_rows, cols)
            right = full[:, n].reshape(cols, full.shape[3])
            acc[...] += jnp.dot(left, right, preferred_element_type=jnp.float32)

    drive(0, 5)
    gather_last(1)
    gather_partner(1)
    shock_up(up_source(4), 0).wait_recv()
    shock_down(down_source(4), 1).wait_recv()
    drive(5, 8)

    def scatter(src, dst, lane, d):
        to = lax.rem(me + d, group)
        return push(
            src.at[to], dst.at[me], t_send.at[lane * group + to], t_recv.at[lane * group + me],
            {"path": to},
        )

    def share(src, lane, d):
        to = lax.rem(me + d, group)
        return push(
            src.at[me], src.at[me], t_send.at[lane * group + to], t_recv.at[lane * group + me],
            {"path": to},
        )

    def taken(dst, lane, d):
        source = lax.rem(me + d, group)
        return push(
            dst.at[source], dst.at[source], t_send.at[lane * group + source],
            t_recv.at[lane * group + source], {"path": source},
        )

    def each(action):
        @pl.loop(1, group)
        def _(d):
            action(d)

    contract = (((0,), (0,)), ((), ()))
    rows = nb // 8
    w = jnp.zeros((paths, nb), jnp.float32)
    for t in range(steps):
        here = pl.ds(t * paths, paths)
        w = w + (acc[here, sets : sets + nb] + acc[here, sets + nb : sets + 2 * nb])
        basis = jnp.tanh(w)
        base[t] = basis
        gram = lax.dot_general(
            basis, basis, contract, precision=HIGH, preferred_element_type=jnp.float32
        )
        gram = jnp.concatenate([gram, jnp.zeros_like(gram)], axis=1)
        gram_part[t * rows : (t + 1) * rows] = gram.reshape(rows, 8, 2 * nb)
    each(lambda d: scatter(gram_part, gram_in, 0, d).start())
    gram_in[me] = gram_part[me]

    v = jnp.zeros((paths, sets), jnp.float32)
    for t in range(steps):
        v = v + acc[pl.ds(t * paths, paths), 0:sets]
        values = jnp.maximum(v, 0.0) + jnp.log(1.0 + jnp.exp(-jnp.abs(v))) - 1.0
        moment = lax.dot_general(
            base[t], values, contract, precision=HIGH, preferred_element_type=jnp.float32
        )
        part[t * rows : (t + 1) * rows] = moment.reshape(rows, 8, sets)
    each(lambda d: scatter(part, landed, 1, d).start())
    landed[me] = part[me]

    each(lambda d: taken(gram_in, 0, d).wait_recv())
    gram_sum[me] = jnp.sum(gram_in[...], axis=0)
    each(lambda d: share(gram_sum, 2, d).start())

    each(lambda d: taken(landed, 1, d).wait_recv())
    member = (
        lax.broadcasted_iota(jnp.int32, (sets, set_ref.shape[1]), 0) == lax.rem(set_ref[...], sets)
    ).astype(jnp.float32).astype(jnp.bfloat16)
    total[me] = split_dot(jnp.sum(landed[...], axis=0), member)
    each(lambda d: share(total, 3, d).start())

    each(lambda d: taken(gram_sum, 2, d).wait_recv())
    row = lax.broadcasted_iota(jnp.int32, (nb, nb), 0)
    lane = lax.broadcasted_iota(jnp.int32, (nb, nb), 1)
    ridge = jnp.where(row == lane, 0.01 * total_paths, 0.0)
    inverses = invert(
        [
            gram_sum[t * rows : (t + 1) * rows, :, 0:nb].reshape(nb, nb) + ridge
            for t in range(steps)
        ]
    )
    weights = [
        jnp.dot(base[t], inverses[t], precision=HIGH, preferred_element_type=jnp.float32)
        for t in range(steps)
    ]
    each(lambda d: taken(total, 3, d).wait_recv())
    for t in range(steps):
        moment = total[t * rows : (t + 1) * rows].reshape(nb, sets)
        predicted = jnp.dot(
            weights[t], moment, precision=HIGH, preferred_element_type=jnp.float32
        )
        out_ref[t] = jnp.maximum(predicted, 0.0)

    each(lambda d: scatter(gram_part, gram_in, 0, d).wait_send())
    each(lambda d: scatter(part, landed, 1, d).wait_send())
    each(lambda d: share(gram_sum, 2, d).wait_send())
    each(lambda d: share(total, 3, d).wait_send())
    for copy in sent:
        copy.wait_send()
    for k in range(0, 4):
        for h in range(2):
            if k < 3 or h == 0:
                shock_up(up_source(k), h).wait_send()
            if k < 3 or h == 1:
                shock_down(down_source(k), h).wait_send()

    @pl.loop(1, planes)
    def _(d):
        vol_copy(d).wait_send()

    @pl.when(me >= per_plane * z)
    def _():
        each(lambda d: slice_copy(d).wait_send())

    @pl.loop(0, 4)
    def _(k):
        low, high = up_source(k), down_source(k)
        rise, fall = rises(low), planes - 1 - rises(high)

        @pl.loop(0, planes)
        def _(g):
            @pl.when((g >= low) & (k < rise))
            def _():
                slice_up(low, g).wait_send()

            @pl.when((g >= high) & (k < fall))
            def _():
                slice_down(high, g).wait_send()


def on_device(shocks, chol_factor, factor_vol, trade_loading, basis_loading, trade_set):
    steps, paths, cols = shocks.shape
    planes, group = lax.axis_size("fac"), lax.axis_size("path")
    rows = steps * paths
    height = chol_factor.shape[0]
    width = cols // group
    total, sets = trade_loading.shape
    nb = basis_loading.shape[1]
    wide = sets + 2 * nb
    vmem = pl.BlockSpec(memory_space=pltpu.VMEM)
    hbm = pl.BlockSpec(memory_space=pl.ANY)
    dma = pltpu.SemaphoreType.DMA
    return pl.pallas_call(
        functools.partial(
            kernel, planes, group, 1.0 / math.sqrt(steps), paths * group
        ),
        out_shape=jax.ShapeDtypeStruct((steps, paths, sets), jnp.float32),
        in_specs=[hbm, hbm, vmem, hbm, hbm, vmem],
        out_specs=vmem,
        scratch_shapes=[
            pltpu.VMEM(chol_factor.shape, jnp.bfloat16),
            pltpu.VMEM((nb, total), jnp.bfloat16),
            pltpu.VMEM((group, width, height), jnp.bfloat16),
            pltpu.VMEM((group, planes, width, height), jnp.bfloat16),
            pltpu.VMEM((planes, 2, rows // 2, cols), jnp.bfloat16),
            pltpu.VMEM((planes, cols // 128, 128), jnp.float32),
            pltpu.VMEM((total, wide), jnp.bfloat16),
            pltpu.VMEM((group, planes, width, wide), jnp.bfloat16),
            pltpu.VMEM((rows, wide), jnp.float32),
            pltpu.VMEM((group, 8, 2 * nb), jnp.float32),
            pltpu.VMEM((group, 8, 2 * nb), jnp.float32),
            pltpu.VMEM((group, 8, 2 * nb), jnp.float32),
            pltpu.VMEM((group, 8, sets), jnp.float32),
            pltpu.VMEM((group, 8, sets), jnp.float32),
            pltpu.VMEM((group, 8, sets), jnp.float32),
            pltpu.VMEM((steps, paths, nb), jnp.float32),
            dma((5,)),
            dma((group,)),
            dma((group,)),
            dma((planes,)),
            dma((planes,)),
            dma((2 * planes,)),
            dma((2 * planes,)),
            dma((2 * planes,)),
            dma((planes * planes,)),
            dma((planes * planes,)),
            dma((planes * planes,)),
            dma((128,)),
            dma((4 * group,)),
            dma((4 * group,)),
            dma((4 * group,)),
        ],
        compiler_params=pltpu.CompilerParams(
            collective_id=0, has_side_effects=True, vmem_limit_bytes=62 * 2**20
        ),
    )(
        chol_factor,
        shocks.reshape(rows, cols),
        factor_vol.reshape(-1, 128),
        trade_loading,
        basis_loading.T,
        trade_set.reshape(1, -1),
    )


def solution(mesh):
    in_specs = (P(None, "path", "fac"), P("path", "fac"), P("fac"), P(None, "fac"), P(), P("fac"))
    out_specs = P(None, "path", "fac")
    return jax.shard_map(
        on_device, mesh=mesh, in_specs=in_specs, out_specs=out_specs, check_vma=False
    )
```
